32 devices in a mesh: wide: 16 (over z, y, x), lev: 2 (over core).
Axes of the slice: x: 2, y: 2, z: 4, core: 2. Of those that a mesh axis runs over, the one named last changes fastest.
Arguments:
- alpha: bfloat16 [16, 4, 64, 1024], P('wide', None, 'lev'), may hold values from -6 to 6
- ens: bfloat16 [16, 4, 64, 1024], P('wide', None, 'lev'), may hold values from -6 to 6
- htile: bfloat16 [8, 128, 128], replicated, may hold values from -0.1875 to 0.1875
- vloc: float32 [64, 9], replicated, may hold values from 0.1 to 0.55
- pattern: int32 [8, 8], replicated, may hold values from 0 to 7
- region_sizes: int32 [16], replicated, may hold values from 1 to 128, 1024 in all
- owner: int32 [16], replicated, may hold values from 0 to 15, each once
- cotangent: bfloat16 [4, 64, 2048], P(None, 'lev', 'wide'), may hold values from -6 to 6
Outputs:
- increment: bfloat16 [4, 64, 2048], P(None, 'lev', 'wide')
- gradient: bfloat16 [16, 4, 64, 1024], P('wide', None, 'lev')
The draws below stay inside these ranges and needn't reach their ends.
Inputs may be any that keep to these rules, and one draw needn't show every extreme that they name: `region_sizes`: the entries sum to 1024; the largest equals 128. `owner`: each index of wide appears once. `pattern`: entries of a row may repeat.
All inputs are finite; a program needn't handle non-finite values.
Results may differ from the reference program's by a relative error of at most 0.008.
Values may be sent and summed in bfloat16 or wider, within the bound.
No kernel may reach another device: no remote copies, remote signals or barrier semaphores. Data moves between devices by JAX's collectives and lax.ppermute only.
A program may use at most 128 MiB of HBM per device.

```python
import math
import jax
import jax.numpy as jnp
import numpy as np
from jax import lax

F = 4
LEV = 64
VREACH = 4
BLK = 128
KB = 8
MEM = 16
COLS = 1024
RMAX = 128
NB = 8
N_WIDE = 16


def set_ends(result, own_key, least, top_value):
    place = [jax.random.randint(jax.random.fold_in(own_key, axis), (), 0, length) for axis, length in enumerate(result.shape)]
    main_axis = result.shape.index(max(result.shape))
    next_to = place[:main_axis] + [(place[main_axis] + 1) % result.shape[main_axis]] + place[main_axis + 1:]
    return result.at[tuple(place)].set(least).at[tuple(next_to)].set(top_value)


def with_spikes(drawn, key, source, target, parts, factor):
    owner, partner = [(jnp.arange(drawn.shape[axis_at]) // (drawn.shape[axis_at] // parts)).reshape([-1 if axis == axis_at else 1 for axis in range(drawn.ndim)]) for axis_at in (source, target)]
    chosen = jax.random.permutation(key, parts)[partner]
    strong = (owner == chosen) | (owner == (partner + parts // 2) % parts)
    return jnp.where(strong, factor * drawn, drawn)


def block_scale(own_key, dims, pieces, least, high):
    def one(dim, blocks):
        heights = jax.random.uniform(jax.random.fold_in(jax.random.fold_in(own_key, 6), dim), (blocks,), jnp.float32, least / len(pieces), high / len(pieces))
        return jnp.repeat(jnp.exp(heights), dims[dim] // blocks).reshape((-1,) + (1,) * (len(dims) - dim - 1))

    loudness = one(*pieces[0])
    for cut in pieces[1:]:
        loudness = loudness * one(*cut)
    return loudness


def profile(count, total, limit, skew):
    weights = [(1 << 20) // math.isqrt(rank ** skew) + 1 for rank in range(2, count + 1)]
    rest, counts = total - limit - (count - 1), [1] * (count - 1)
    while rest > 0:
        free = [i for i in range(count - 1) if counts[i] < limit]
        whole, budget = sum([weights[i] for i in free]), rest
        for i in free:
            addition = min(limit - counts[i], max(1, budget * weights[i] // whole), rest)
            counts[i] = counts[i] + addition
            rest = rest - addition
    return np.array([limit] + counts)


def uneven_parts(key, number_of, total, bound, skew):
    if number_of == 2:
        one = jax.random.randint(key, (), max(1, total - bound), min(bound, total - 1) + 1)
        return jnp.stack([one, total - one])
    tallies = jnp.asarray(profile(number_of, total, bound, skew), jnp.int32)
    twos = (number_of - 1) // 2
    donor, receiver = tallies[1:1 + 2 * twos:2], tallies[2:2 + 2 * twos:2]
    room = jnp.minimum(donor - 1, bound - receiver)
    passed = jax.random.randint(jax.random.fold_in(key, 1), (twos,), 0, 1 << 20) % (room + 1)
    tallies = tallies.at[1:1 + 2 * twos:2].set(donor - passed).at[2:2 + 2 * twos:2].set(receiver + passed)
    return tallies[jax.random.permutation(jax.random.fold_in(key, 2), number_of)]


def centred(stream_key, dims, scale, most, pieces=(), kind=jnp.bfloat16):
    factor_of = block_scale(stream_key, dims, pieces, -0.22, 0.18) if pieces else 1.0
    entries = jax.random.normal(stream_key, dims, jnp.float32) * scale * factor_of
    return jnp.minimum(jnp.maximum(entries, -most), most).astype(kind)


def noise_with(own_key, extent, width, reach, shards, heavy, held_as=jnp.bfloat16):
    result = width * jax.random.normal(own_key, extent, jnp.float32)
    if shards:
        result = result * block_scale(own_key, extent, shards, -0.22, 0.18)
    return jnp.clip(with_spikes(result, jax.random.fold_in(own_key, 3), *heavy), -reach, reach).astype(held_as)


def setup_inputs(seed: int = 0) -> dict:
    key_of = jax.random.split(jax.random.key(seed), 9)
    alpha = centred(key_of[0], (MEM, F, LEV, COLS), 1.0, 6.0, ((0, 16), (2, 2)))
    ens = noise_with(key_of[1], (MEM, F, LEV, COLS), 1.0, 6.0, ((0, 16), (2, 2)), (0, 3, 16, 2.0))
    htile = centred(key_of[2], (KB, BLK, BLK), (KB * BLK) ** -0.5, 0.1875)
    vloc = jnp.clip(jax.random.uniform(key_of[3], (LEV, 2 * VREACH + 1), jnp.float32, 0.1, 0.55), 0.1, 0.55)
    pattern = set_ends(jax.random.randint(key_of[4], (NB, KB), 0, NB), jax.random.fold_in(key_of[4], 1), 0, NB - 1).astype(jnp.int32)
    region_sizes = uneven_parts(key_of[5], N_WIDE, COLS, RMAX, 2).astype(jnp.int32)
    owner = jax.random.permutation(key_of[6], N_WIDE).astype(jnp.int32)
    cotangent = centred(key_of[7], (F, LEV, N_WIDE * RMAX), 1.0, 6.0, ((1, 2), (2, 16)))
    return dict(alpha=alpha, ens=ens, htile=htile, vloc=vloc, pattern=pattern, region_sizes=region_sizes, owner=owner, cotangent=cotangent)


def slot_table(region_sizes, owner):
    region_ends = jnp.cumsum(region_sizes).astype(jnp.int32)
    region_starts = (region_ends - region_sizes).astype(jnp.int32)
    column_ids = jnp.arange(COLS, dtype=jnp.int32)
    region_of = lax.optimization_barrier(jnp.sum((region_ends[None, :] <= column_ids[:, None]).astype(jnp.int32), axis=1))
    return (owner[region_of] * RMAX + column_ids - region_starts[region_of]).astype(jnp.int32)

def spread(values, pattern, htile):
    flat_rows = values.reshape(F * LEV, NB, BLK)
    summed = jnp.zeros((F * LEV * NB, BLK), jnp.float32)
    for k in range(KB):
        picked = jnp.take(flat_rows, pattern[:, k], axis=1).reshape(F * LEV * NB, BLK)
        summed = summed + jnp.dot(picked, htile[k], preferred_element_type=jnp.float32)
    return summed.reshape(F, LEV, COLS).astype(jnp.bfloat16)

def gather_back(values, pattern, htile):
    moved = jnp.moveaxis(values.reshape(F * LEV, NB, BLK).astype(jnp.float32), 1, 0)
    summed = jnp.zeros((F * LEV * NB, BLK), jnp.float32)
    for k in range(KB):
        selected = jax.ops.segment_sum(moved, pattern[:, k], num_segments=NB).astype(jnp.bfloat16)
        selected = jnp.moveaxis(selected, 0, 1).reshape(F * LEV * NB, BLK)
        summed = summed + jnp.dot(selected, htile[k].T, preferred_element_type=jnp.float32)
    return summed.reshape(F, LEV, COLS).astype(jnp.bfloat16)

def vertical(values, vloc):
    padded = jnp.pad(values.astype(jnp.float32), ((0, 0), (VREACH, VREACH), (0, 0)))
    summed = jnp.zeros(values.shape, jnp.float32)
    for offset in range(-VREACH, VREACH + 1):
        weight = vloc[:, offset + VREACH]
        summed = summed + weight[None, :, None] * padded[:, VREACH + offset:VREACH + offset + LEV, :]
    return summed.astype(jnp.bfloat16)

def vertical_adjoint(values, vloc):
    padded = jnp.pad(values.astype(jnp.float32), ((0, 0), (VREACH, VREACH), (0, 0)))
    vpadded = jnp.pad(vloc, ((VREACH, VREACH), (0, 0)))
    summed = jnp.zeros(values.shape, jnp.float32)
    for offset in range(-VREACH, VREACH + 1):
        weight = vpadded[VREACH - offset:VREACH - offset + LEV, offset + VREACH]
        summed = summed + weight[None, :, None] * padded[:, VREACH - offset:VREACH - offset + LEV, :]
    return summed.astype(jnp.bfloat16)

def reference(alpha, ens, htile, vloc, pattern, region_sizes, owner, cotangent):
    slot_of = slot_table(region_sizes, owner)

    def forward(running, member_pair):
        alpha_one, ens_one = member_pair
        localized = vertical(spread(alpha_one, pattern, htile), vloc)
        return (running + ens_one.astype(jnp.float32) * localized.astype(jnp.float32), None)
    summed, _ = lax.scan(forward, jnp.zeros((F, LEV, COLS), jnp.float32), (alpha, ens))
    column_sum = summed * (1.0 / math.sqrt(MEM))
    increment = jnp.zeros((F, LEV, N_WIDE * RMAX), jnp.float32).at[:, :, slot_of].set(column_sum)
    increment = increment.astype(jnp.bfloat16)
    cot_cols = cotangent[:, :, slot_of]

    def backward(ens_one):
        scaled = (ens_one.astype(jnp.float32) * cot_cols.astype(jnp.float32)).astype(jnp.bfloat16)
        adjoint_mix = vertical_adjoint(scaled, vloc)
        return gather_back(adjoint_mix, pattern, htile)
    gradient = lax.map(backward, ens)
    return (increment, gradient)
```

```python
import functools
import math

import jax
import jax.numpy as jnp
from jax import lax
from jax.experimental import pallas as pl
from jax.experimental.pallas import tpu as pltpu
from jax.sharding import PartitionSpec as P

VREACH = 4
SUB = 8
VMEM = pl.BlockSpec(memory_space=pltpu.VMEM)
SMEM = pl.BlockSpec(memory_space=pltpu.SMEM)


def halo_swap(rows_top, rows_bottom, axis):
    count = lax.axis_size(axis)
    if count == 2:
        both = lax.ppermute(
            jnp.stack([rows_top, rows_bottom]), axis, [(0, 1), (1, 0)]
        )
        return both[0], both[1]
    below = lax.ppermute(rows_top, axis, [(i, i + 1) for i in range(count - 1)])
    above = lax.ppermute(rows_bottom, axis, [(i + 1, i) for i in range(count - 1)])
    return below, above


def split_bf16(value):
    high = value.astype(jnp.bfloat16)
    return high, (value - high.astype(jnp.float32)).astype(jnp.bfloat16)


def weight_kernel(fields, slabs, vloc_ref, down_ref, up_ref, padded):
    reach = VREACH
    levels_all = vloc_ref.shape[0]
    levels = levels_all // slabs
    rows = fields * levels
    halo = fields * reach
    slab = lax.axis_index("lev")
    padded[...] = jnp.zeros_like(padded)
    padded[SUB : SUB + levels_all, :] = vloc_ref[...]
    window = padded[pl.ds(pl.multiple_of(slab * levels, SUB), levels + 2 * SUB), :]
    own = jnp.concatenate([window[SUB : SUB + levels]] * fields, axis=0)
    below = jnp.concatenate([window[SUB - reach : SUB]] * fields, axis=0)
    above = jnp.concatenate([window[SUB + levels : SUB + levels + reach]] * fields, axis=0)

    def iota(shape, dim):
        return lax.broadcasted_iota(jnp.int32, shape, dim)

    def band(weights, shift, same):
        total = jnp.zeros(shift.shape, jnp.float32)
        for tap in range(2 * reach + 1):
            column = jnp.broadcast_to(weights[:, tap : tap + 1], shift.shape)
            total = jnp.where((shift == tap - reach) & same, column, total)
        return total

    row, col = iota((rows, rows), 0), iota((rows, rows), 1)
    same = (row // levels) == (col // levels)
    inner = band(own, col - row, same)

    row, col = iota((rows, halo), 0), iota((rows, halo), 1)
    same = (row // levels) == (col // reach)
    level, step = row % levels, col % reach
    low = band(own, step - reach - level, same & (slab > 0))
    high = band(own, levels + step - level, same & (slab < slabs - 1))
    for part, (start, stop) in (
        (inner, (0, rows)),
        (low, (rows, rows + halo)),
        (high, (rows + halo, rows + 2 * halo)),
    ):
        first, second = split_bf16(part)
        down_ref[0, :, start:stop] = first
        down_ref[1, :, start:stop] = second

    row, col = iota((halo, rows), 0), iota((halo, rows), 1)
    same = (row // reach) == (col // levels)
    step, level = row % reach, col % levels
    low = band(below, level - (step - reach), same & (slab > 0))
    high = band(above, level - (levels + step), same & (slab < slabs - 1))
    for part, (start, stop) in (
        (inner, (0, rows)),
        (low, (rows, rows + halo)),
        (high, (rows + halo, rows + 2 * halo)),
    ):
        first, second = split_bf16(part)
        up_ref[0, start:stop, :] = first
        up_ref[1, start:stop, :] = second


def region_loop(sizes_ref, owner_ref, width, body):
    def step(region, start):
        size = sizes_ref[region]
        body(owner_ref[region], start // width, start % width, size)
        return start + size

    lax.fori_loop(0, sizes_ref.shape[0], step, jnp.int32(0), unroll=4)


def forward_kernel(
    inner, pattern_ref, sizes_ref, owner_ref, alpha_ref, halo_ref, down_ref, ens_ref, htile_ref,
    out_ref, mixed, product,
):
    blocks, slots = pattern_ref.shape
    rows = alpha_ref.shape[0]
    width = htile_ref.shape[1]
    span = rows + halo_ref.shape[0]
    extended = jnp.concatenate([alpha_ref[...], halo_ref[...]], axis=0)
    summed = jnp.dot(down_ref[0], extended, preferred_element_type=jnp.float32)
    summed = summed + jnp.dot(down_ref[1], extended, preferred_element_type=jnp.float32)
    for b in range(blocks):
        mixed[b] = summed[:, b * width : (b + 1) * width].astype(jnp.bfloat16)

    def spread(b, carry):
        picked = jnp.concatenate([mixed[pattern_ref[b, k]] for k in range(slots)], axis=1)
        localized = jnp.dot(picked, htile_ref[...], preferred_element_type=jnp.float32)
        columns = pl.ds(pl.multiple_of(b * width, width), width)
        product[b] = localized * ens_ref[:, columns].astype(jnp.float32)
        return carry

    lax.fori_loop(0, blocks, spread, 0, unroll=min(blocks, 8))
    product[blocks] = jnp.zeros((rows, width), jnp.float32)
    lane = lax.broadcasted_iota(jnp.int32, (rows, width), 1)

    def place(owner, block, shift, size):
        both = jnp.where(lane >= shift, product[block], product[block + 1])
        turned = pltpu.roll(both, (width - shift) % width, 1)
        kept = jnp.where(lane < size, turned, 0.0)
        out_ref[owner % inner, owner // inner] = kept.astype(jnp.bfloat16)

    region_loop(sizes_ref, owner_ref, width, place)


def scale_kernel(
    inner, sizes_ref, owner_ref, cot_ref, ens_ref, out_ref, columns_of
):
    width = cot_ref.shape[3]
    rows = ens_ref.shape[0]
    blocks = ens_ref.shape[1] // width
    lane = lax.broadcasted_iota(jnp.int32, (rows, width), 1)
    columns_of[0] = jnp.zeros((rows, width), jnp.float32)

    def place(owner, block, shift, size):
        region = cot_ref[owner % inner, owner // inner].astype(jnp.float32)
        turned = pltpu.roll(region, shift, 1)
        columns_of[block] = jnp.where(lane >= shift, turned, columns_of[block])
        columns_of[block + 1] = turned

    region_loop(sizes_ref, owner_ref, width, place)
    for b in range(blocks):
        part = slice(b * width, (b + 1) * width)
        out_ref[:, part] = (ens_ref[:, part].astype(jnp.float32) * columns_of[b]).astype(
            jnp.bfloat16
        )


def backward_kernel(
    pattern_ref, scaled_ref, halo_ref, up_ref, htile_ref, out_ref, mixed, total
):
    blocks, slots = pattern_ref.shape
    rows = scaled_ref.shape[0]
    width = htile_ref.shape[1]
    extended = jnp.concatenate([scaled_ref[...], halo_ref[...]], axis=0)
    dims = (((0,), (0,)), ((), ()))
    summed = lax.dot_general(up_ref[0], extended, dims, preferred_element_type=jnp.float32)
    summed = summed + lax.dot_general(
        up_ref[1], extended, dims, preferred_element_type=jnp.float32
    )
    for b in range(blocks):
        mixed[b] = summed[:, b * width : (b + 1) * width].astype(jnp.bfloat16)
        total[b] = jnp.zeros((rows, width), jnp.float32)

    def gather(b, carry):
        spread = lax.dot_general(
            mixed[b], htile_ref[...], (((1,), (1,)), ((), ())), preferred_element_type=jnp.float32
        )
        for k in range(slots):
            target = pattern_ref[b, k]
            total[target] = total[target] + spread[:, k * width : (k + 1) * width]
        return carry

    lax.fori_loop(0, blocks, gather, 0, unroll=min(blocks, 8))
    for b in range(blocks):
        out_ref[:, b * width : (b + 1) * width] = total[b].astype(jnp.bfloat16)


def sum_kernel(scale, parts_ref, out_ref):
    total = parts_ref[0].astype(jnp.float32)
    for i in range(1, parts_ref.shape[0]):
        total = total + parts_ref[i].astype(jnp.float32)
    out_ref[...] = (total * scale).astype(jnp.bfloat16)


def body(alpha, ens, htile, vloc, pattern, region_sizes, owner, cotangent):
    reach = VREACH
    members, fields, levels, columns = alpha.shape
    assert members == 1
    slots, width, _ = htile.shape
    blocks = columns // width
    region_max = cotangent.shape[2]
    assert region_max == width
    wide = lax.axis_size("wide")
    slabs = lax.axis_size("lev")
    inner = next(i for i in range(math.isqrt(wide), wide + 1) if wide % i == 0)
    outer = wide // inner
    lines = [[o * inner + i for o in range(outer)] for i in range(inner)]
    planes = [[o * inner + i for i in range(inner)] for o in range(outer)]
    rows = fields * levels
    halo = fields * reach
    member_scale = 1.0 / math.sqrt(members * wide)

    cot_rows = cotangent.reshape(1, rows, region_max)
    cot_line = lax.all_to_all(
        jnp.broadcast_to(cot_rows, (outer, rows, region_max)),
        "wide", 0, 0, axis_index_groups=lines, tiled=True,
    )

    def halo_of(block):
        below, above = halo_swap(
            block[:, levels - reach :, :].reshape(halo, columns),
            block[:, :reach, :].reshape(halo, columns),
            "lev",
        )
        return jnp.concatenate([below, above], axis=0)

    alpha_rows = alpha.reshape(rows, columns)
    ens_rows = ens.reshape(rows, columns)
    stacked = htile.reshape(slots * width, width)
    span = rows + 2 * halo
    down, up = pl.pallas_call(
        functools.partial(weight_kernel, fields, slabs),
        out_shape=(
            jax.ShapeDtypeStruct((2, rows, span), jnp.bfloat16),
            jax.ShapeDtypeStruct((2, span, rows), jnp.bfloat16),
        ),
        in_specs=[VMEM],
        out_specs=(VMEM, VMEM),
        scratch_shapes=[pltpu.VMEM((vloc.shape[0] + 2 * SUB, vloc.shape[1]), jnp.float32)],
        name="weights",
    )(vloc)

    products = pl.pallas_call(
        functools.partial(forward_kernel, inner),
        out_shape=jax.ShapeDtypeStruct((inner, outer, rows, width), jnp.bfloat16),
        in_specs=[SMEM] * 3 + [VMEM] * 5,
        out_specs=VMEM,
        scratch_shapes=[
            pltpu.VMEM((blocks, rows, width), jnp.bfloat16),
            pltpu.VMEM((blocks + 1, rows, width), jnp.float32),
        ],
        cost_estimate=pl.CostEstimate(flops=10**9, bytes_accessed=2 << 20, transcendentals=0),
        name="forward",
    )(pattern, region_sizes, owner, alpha_rows, halo_of(alpha[0]), down, ens_rows, stacked)

    merged = jnp.concatenate(
        [products, jnp.broadcast_to(cot_line[None], (inner,) + cot_line.shape)], axis=1
    )
    arrived = lax.all_to_all(merged, "wide", 0, 0, axis_index_groups=planes, tiled=True)
    partial = pl.pallas_call(
        functools.partial(sum_kernel, 1.0),
        grid=(1,),
        out_shape=jax.ShapeDtypeStruct((outer, rows, width), jnp.bfloat16),
        in_specs=[pl.BlockSpec((inner, outer, rows, width), lambda i: (0, 0, 0, 0))],
        out_specs=pl.BlockSpec((outer, rows, width), lambda i: (0, 0, 0)),
        name="partial",
    )(arrived)
    terms = lax.all_to_all(partial, "wide", 0, 0, axis_index_groups=lines, tiled=True)

    scaled = pl.pallas_call(
        functools.partial(scale_kernel, inner),
        grid=(1,),
        out_shape=jax.ShapeDtypeStruct((rows, columns), jnp.bfloat16),
        in_specs=[
            SMEM,
            SMEM,
            pl.BlockSpec((inner, outer, rows, width), lambda i: (0, 1, 0, 0)),
            pl.BlockSpec((rows, columns), lambda i: (0, 0)),
        ],
        out_specs=pl.BlockSpec((rows, columns), lambda i: (0, 0)),
        scratch_shapes=[pltpu.VMEM((blocks + 1, rows, width), jnp.float32)],
        cost_estimate=pl.CostEstimate(flops=10**7, bytes_accessed=1 << 20, transcendentals=0),
        name="scale",
    )(region_sizes, owner, arrived, ens_rows)
    gradient = pl.pallas_call(
        backward_kernel,
        out_shape=jax.ShapeDtypeStruct((rows, columns), jnp.bfloat16),
        in_specs=[SMEM] + [VMEM] * 4,
        out_specs=VMEM,
        scratch_shapes=[
            pltpu.VMEM((blocks, rows, width), jnp.bfloat16),
            pltpu.VMEM((blocks, rows, width), jnp.float32),
        ],
        cost_estimate=pl.CostEstimate(flops=10**9, bytes_accessed=1 << 20, transcendentals=0),
        name="backward",
    )(pattern, scaled, halo_of(scaled.reshape(fields, levels, columns)), up, stacked)

    increment = pl.pallas_call(
        functools.partial(sum_kernel, member_scale),
        out_shape=jax.ShapeDtypeStruct((rows, width), jnp.bfloat16),
        in_specs=[VMEM],
        out_specs=VMEM,
        name="total",
    )(terms)
    return (
        increment.reshape(fields, levels, width),
        gradient.reshape(members, fields, levels, columns),
    )


def solution(mesh):
    placed = (
        P("wide", None, "lev", None),
        P("wide", None, "lev", None),
        P(),
        P(),
        P(),
        P(),
        P(),
        P(None, "lev", "wide"),
    )
    return jax.shard_map(
        body,
        mesh=mesh,
        in_specs=placed,
        out_specs=(P(None, "lev", "wide"), P("wide", None, "lev", None)),
        check_vma=False,
    )
```

```python
import functools
import math

import jax
import jax.numpy as jnp
from jax import lax
from jax.experimental import pallas as pl
from jax.experimental.pallas import tpu as pltpu
from jax.sharding import PartitionSpec as P


VREACH = 4
LANES = 128
VMEM = pl.BlockSpec(memory_space=pltpu.VMEM)
SMEM = pl.BlockSpec(memory_space=pltpu.SMEM)


def neighbour_slabs(block):
    count = lax.axis_size("lev")
    if count == 2:
        return [lax.ppermute(block, "lev", [(0, 1), (1, 0)])]
    return [
        lax.ppermute(block, "lev", [(i, i + 1) for i in range(count - 1)]),
        lax.ppermute(block, "lev", [(i + 1, i) for i in range(count - 1)]),
    ]


def slab_steps(slabs):
    if slabs == 2:
        return [0, 1 - 2 * lax.axis_index("lev")]
    return [0, -1, 1]


def split_bf16(value):
    high = value.astype(jnp.bfloat16)
    return high, (value - high.astype(jnp.float32)).astype(jnp.bfloat16)


def weight_kernel(fields, slabs, vloc_ref, down_ref, up_ref, taps):
    slab = lax.axis_index("lev")
    reach = VREACH
    levels = vloc_ref.shape[1] // slabs
    rows = fields * levels
    taps[...] = jnp.zeros_like(taps)
    taps[: vloc_ref.shape[0], : vloc_ref.shape[1]] = vloc_ref[...]
    lane = lax.broadcasted_iota(jnp.int32, taps.shape, 1)

    def slab_weights(step):
        first = (slab + step) * levels
        turned = pltpu.roll(taps[...], lax.rem(2 * LANES - first, LANES), 1)
        once = jnp.where(lane < levels, turned, 0.0)
        total = once
        for field in range(1, fields):
            total = total + pltpu.roll(once, field * levels, 1)
        return total

    row = lax.broadcasted_iota(jnp.int32, (rows, rows), 0)
    col = lax.broadcasted_iota(jnp.int32, (rows, rows), 1)
    same = (row // levels) == (col // levels)
    own = slab_weights(0)

    def band(weights, shift, valid):
        total = jnp.zeros((rows, rows), jnp.float32)
        for tap in range(2 * reach + 1):
            line = jnp.broadcast_to(weights[tap : tap + 1, :rows], (rows, rows))
            total = jnp.where(shift == tap - reach, line, total)
        return split_bf16(jnp.where(same & valid, total, 0.0))

    for i, step in enumerate(slab_steps(slabs)):
        valid = (slab + step >= 0) & (slab + step < slabs)
        part = slice(i * rows, (i + 1) * rows)
        offset = step * levels
        down_ref[0, part, :], down_ref[1, part, :] = band(own, row + offset - col, valid)
        up_ref[0, :, part], up_ref[1, :, part] = band(
            own if i == 0 else slab_weights(step), row - col - offset, valid
        )


def region_loop(sizes_ref, owner_ref, width, body):
    def step(region, start):
        size = sizes_ref[region]
        body(owner_ref[region], start // width, start % width, size)
        return start + size

    lax.fori_loop(0, sizes_ref.shape[0], step, jnp.int32(0), unroll=4)


def forward_kernel(grid, pattern_ref, sizes_ref, owner_ref, down_ref, ens_ref, htile_ref, *refs):
    outer, inner = grid
    out_refs = refs[-inner - 3 : -3]
    slab_refs = refs[: -inner - 3]
    mixed, product, placed = refs[-3:]
    blocks, slots = pattern_ref.shape
    rows = ens_ref.shape[0]
    width = htile_ref.shape[1]
    extended = jnp.concatenate([ref[...] for ref in slab_refs], axis=0)
    dims = (((0,), (0,)), ((), ()))
    summed = lax.dot_general(down_ref[0], extended, dims, preferred_element_type=jnp.float32)
    summed = summed + lax.dot_general(
        down_ref[1], extended, dims, preferred_element_type=jnp.float32
    )
    for b in range(blocks):
        mixed[b] = summed[:, b * width : (b + 1) * width].astype(jnp.bfloat16)

    def spread(b, carry):
        picked = jnp.concatenate([mixed[pattern_ref[b, k]] for k in range(slots)], axis=1)
        localized = jnp.dot(picked, htile_ref[...], preferred_element_type=jnp.float32)
        columns = pl.ds(pl.multiple_of(b * width, width), width)
        product[b] = localized * ens_ref[:, columns].astype(jnp.float32)
        return carry

    lax.fori_loop(0, blocks, spread, 0, unroll=min(blocks, 8))
    product[blocks] = jnp.zeros((rows, width), jnp.float32)
    lane = lax.broadcasted_iota(jnp.int32, (rows, width), 1)
    me = lax.axis_index("wide")
    here, line = me % inner, me // inner

    def place(owner, block, shift, size):
        both = jnp.where(lane >= shift, product[block], product[block + 1])
        turned = pltpu.roll(both, (width - shift) % width, 1)
        kept = jnp.where(lane < size, turned, 0.0).astype(jnp.bfloat16)
        placed[(owner % inner - here + inner) % inner, (owner // inner - line + outer) % outer] = kept

    region_loop(sizes_ref, owner_ref, width, place)
    for i in range(inner):
        out_refs[i][...] = placed[i]


def scale_kernel(grid, sizes_ref, owner_ref, ens_ref, *refs):
    outer, inner = grid
    cot_refs = refs[:inner]
    out_ref, gathered, columns_of = refs[inner:]
    rows, width = cot_refs[0].shape[1:]
    blocks = ens_ref.shape[1] // width
    lane = lax.broadcasted_iota(jnp.int32, (rows, width), 1)
    me = lax.axis_index("wide")
    here, line = me % inner, me // inner
    for i in range(inner):
        gathered[i] = cot_refs[i][...]
    columns_of[0] = jnp.zeros((rows, width), jnp.float32)

    def place(owner, block, shift, size):
        region = gathered[(here - owner % inner + inner) % inner, (line - owner // inner + outer) % outer]
        turned = pltpu.roll(region.astype(jnp.float32), shift, 1)
        columns_of[block] = jnp.where(lane >= shift, turned, columns_of[block])
        columns_of[block + 1] = turned

    region_loop(sizes_ref, owner_ref, width, place)
    for b in range(blocks):
        part = slice(b * width, (b + 1) * width)
        out_ref[:, part] = (ens_ref[:, part].astype(jnp.float32) * columns_of[b]).astype(
            jnp.bfloat16
        )


def backward_kernel(pattern_ref, up_ref, htile_ref, *refs):
    slab_refs = refs[:-3]
    out_ref, mixed, total = refs[-3:]
    blocks, slots = pattern_ref.shape
    rows = out_ref.shape[0]
    width = htile_ref.shape[1]
    extended = jnp.concatenate([ref[...] for ref in slab_refs], axis=0)
    summed = jnp.dot(up_ref[0], extended, preferred_element_type=jnp.float32)
    summed = summed + jnp.dot(up_ref[1], extended, preferred_element_type=jnp.float32)
    for b in range(blocks):
        mixed[b] = summed[:, b * width : (b + 1) * width].astype(jnp.bfloat16)
        total[b] = jnp.zeros((rows, width), jnp.float32)

    def gather(b, carry):
        spread = lax.dot_general(
            mixed[b], htile_ref[...], (((1,), (1,)), ((), ())), preferred_element_type=jnp.float32
        )
        for k in range(slots):
            target = pattern_ref[b, k]
            total[target] = total[target] + spread[:, k * width : (k + 1) * width]
        return carry

    lax.fori_loop(0, blocks, gather, 0, unroll=min(blocks, 8))
    for b in range(blocks):
        out_ref[:, b * width : (b + 1) * width] = total[b].astype(jnp.bfloat16)


def partial_kernel(*refs):
    count = refs[0].shape[0]
    parts, outs = refs[:-count], refs[-count:]
    for i in range(count):
        total = parts[0][i].astype(jnp.float32)
        for part in parts[1:]:
            total = total + part[i].astype(jnp.float32)
        outs[i][...] = total.astype(outs[i].dtype)


def total_kernel(scale, *refs):
    total = refs[0][...].astype(jnp.float32)
    for part in refs[1:-1]:
        total = total + part[...].astype(jnp.float32)
    refs[-1][...] = (total * scale).astype(jnp.bfloat16)


def cost(flops, moved):
    return pl.CostEstimate(flops=flops, bytes_accessed=moved, transcendentals=0)


def body(alpha, ens, htile, vloc, pattern, region_sizes, owner, cotangent):
    members, fields, levels, columns = alpha.shape
    assert members == 1
    slots, width, _ = htile.shape
    blocks = columns // width
    assert cotangent.shape[2] == width == LANES
    wide = lax.axis_size("wide")
    slabs = lax.axis_size("lev")
    inner = next(i for i in range(math.isqrt(wide), wide + 1) if wide % i == 0)
    outer = wide // inner
    grid = (outer, inner)
    rows = fields * levels
    span = rows * len(slab_steps(slabs))
    member_scale = 1.0 / math.sqrt(members * wide)
    bf16 = functools.partial(jax.ShapeDtypeStruct, dtype=jnp.bfloat16)

    def along_line(value, step):
        pairs = [
            (o * inner + i, (o + step) % outer * inner + i)
            for o in range(outer)
            for i in range(inner)
        ]
        return lax.ppermute(value, "wide", pairs)

    def in_plane(value, step):
        pairs = [
            (o * inner + i, o * inner + (i + step) % inner)
            for o in range(outer)
            for i in range(inner)
        ]
        return lax.ppermute(value, "wide", pairs)

    alpha_rows = alpha.reshape(rows, columns)
    ens_rows = ens.reshape(rows, columns)
    stacked = htile.reshape(slots * width, width)
    alpha_slabs = [alpha_rows] + neighbour_slabs(alpha_rows)

    cot_rows = cotangent.reshape(rows, width)
    cot_line = jnp.stack([cot_rows] + [along_line(cot_rows, i) for i in range(1, outer)])
    cot_parts = [cot_line] + [in_plane(cot_line, i) for i in range(1, inner)]

    down, up = pl.pallas_call(
        functools.partial(weight_kernel, fields, slabs),
        out_shape=(bf16((2, span, rows)), bf16((2, rows, span))),
        in_specs=[VMEM],
        out_specs=(VMEM, VMEM),
        scratch_shapes=[pltpu.VMEM((2 * 8, LANES), jnp.float32)],
        cost_estimate=cost(10**6, 10**5),
        name="weights",
    )(vloc.T)

    sent = pl.pallas_call(
        functools.partial(forward_kernel, grid),
        out_shape=[bf16((outer, rows, width))] * inner,
        in_specs=[SMEM] * 3 + [VMEM] * (3 + len(alpha_slabs)),
        out_specs=[VMEM] * inner,
        scratch_shapes=[
            pltpu.VMEM((blocks, rows, width), jnp.bfloat16),
            pltpu.VMEM((blocks + 1, rows, width), jnp.float32),
            pltpu.VMEM((inner, outer, rows, width), jnp.bfloat16),
        ],
        cost_estimate=cost(10**9, 2 << 20),
        name="forward",
    )(pattern, region_sizes, owner, down, ens_rows, stacked, *alpha_slabs)

    arrived = [sent[0]] + [in_plane(sent[i], i) for i in range(1, inner)]
    partial = pl.pallas_call(
        partial_kernel,
        out_shape=[bf16((rows, width))] * outer,
        in_specs=[VMEM] * inner,
        out_specs=[VMEM] * outer,
        cost_estimate=cost(10**6, 1 << 20),
        name="partial",
    )(*arrived)
    terms = [partial[0]] + [along_line(partial[i], i) for i in range(1, outer)]

    scaled = pl.pallas_call(
        functools.partial(scale_kernel, grid),
        out_shape=bf16((rows, columns)),
        in_specs=[SMEM] * 2 + [VMEM] * (1 + inner),
        out_specs=VMEM,
        scratch_shapes=[
            pltpu.VMEM((inner, outer, rows, width), jnp.bfloat16),
            pltpu.VMEM((blocks + 1, rows, width), jnp.float32),
        ],
        cost_estimate=cost(10**7, 1 << 20),
        name="scale",
    )(region_sizes, owner, ens_rows, *cot_parts)
    scaled_slabs = [scaled] + neighbour_slabs(scaled)
    gradient = pl.pallas_call(
        backward_kernel,
        out_shape=bf16((rows, columns)),
        in_specs=[SMEM] + [VMEM] * (2 + len(scaled_slabs)),
        out_specs=VMEM,
        scratch_shapes=[
            pltpu.VMEM((blocks, rows, width), jnp.bfloat16),
            pltpu.VMEM((blocks, rows, width), jnp.float32),
        ],
        cost_estimate=cost(10**9, 1 << 20),
        name="backward",
    )(pattern, up, stacked, *scaled_slabs)

    increment = pl.pallas_call(
        functools.partial(total_kernel, member_scale),
        out_shape=bf16((rows, width)),
        in_specs=[VMEM] * outer,
        out_specs=VMEM,
        cost_estimate=cost(10**6, 1 << 18),
        name="total",
    )(*terms)
    return (
        increment.reshape(fields, levels, width),
        gradient.reshape(members, fields, levels, columns),
    )


def solution(mesh):
    placed = (
        P("wide", None, "lev", None),
        P("wide", None, "lev", None),
        P(),
        P(),
        P(),
        P(),
        P(),
        P(None, "lev", "wide"),
    )
    return jax.shard_map(
        body,
        mesh=mesh,
        in_specs=placed,
        out_specs=(P(None, "lev", "wide"), P("wide", None, "lev", None)),
        check_vma=False,
    )
```

```python
import functools
import math

import jax
import jax.numpy as jnp
from jax import lax
from jax.experimental import pallas as pl
from jax.experimental.pallas import tpu as pltpu
from jax.sharding import PartitionSpec as P


VREACH = 4
LANES = 128
VMEM = pl.BlockSpec(memory_space=pltpu.VMEM)
SMEM = pl.BlockSpec(memory_space=pltpu.SMEM)


def neighbour_slabs(block):
    count = lax.axis_size("lev")
    if count == 2:
        return [lax.ppermute(block, "lev", [(0, 1), (1, 0)])]
    return [
        lax.ppermute(block, "lev", [(i, i + 1) for i in range(count - 1)]),
        lax.ppermute(block, "lev", [(i + 1, i) for i in range(count - 1)]),
    ]


def slab_steps(slabs):
    if slabs == 2:
        return [0, 1 - 2 * lax.axis_index("lev")]
    return [0, -1, 1]


def split_bf16(value):
    high = value.astype(jnp.bfloat16)
    return high, (value - high.astype(jnp.float32)).astype(jnp.bfloat16)


def weight_kernel(fields, slabs, vloc_ref, down_ref, up_ref, taps):
    slab = lax.axis_index("lev")
    reach = VREACH
    levels = vloc_ref.shape[1] // slabs
    rows = fields * levels
    taps[...] = jnp.zeros_like(taps)
    taps[: vloc_ref.shape[0], : vloc_ref.shape[1]] = vloc_ref[...]
    lane = lax.broadcasted_iota(jnp.int32, taps.shape, 1)

    def slab_weights(step):
        first = (slab + step) * levels
        turned = pltpu.roll(taps[...], lax.rem(2 * LANES - first, LANES), 1)
        once = jnp.where(lane < levels, turned, 0.0)
        total = once
        for field in range(1, fields):
            total = total + pltpu.roll(once, field * levels, 1)
        return total

    row = lax.broadcasted_iota(jnp.int32, (rows, rows), 0)
    col = lax.broadcasted_iota(jnp.int32, (rows, rows), 1)
    same = (row // levels) == (col // levels)
    own = slab_weights(0)

    def band(weights, shift, valid):
        total = jnp.zeros((rows, rows), jnp.float32)
        for tap in range(2 * reach + 1):
            line = jnp.broadcast_to(weights[tap : tap + 1, :rows], (rows, rows))
            total = jnp.where(shift == tap - reach, line, total)
        return split_bf16(jnp.where(same & valid, total, 0.0))

    for i, step in enumerate(slab_steps(slabs)):
        valid = (slab + step >= 0) & (slab + step < slabs)
        part = slice(i * rows, (i + 1) * rows)
        offset = step * levels
        down_ref[0, part, :], down_ref[1, part, :] = band(own, row + offset - col, valid)
        up_ref[0, :, part], up_ref[1, :, part] = band(
            own if i == 0 else slab_weights(step), row - col - offset, valid
        )


def region_loop(sizes_ref, owner_ref, width, body):
    def step(region, start):
        size = sizes_ref[region]
        body(owner_ref[region], start // width, start % width, size)
        return start + size

    lax.fori_loop(0, sizes_ref.shape[0], step, jnp.int32(0), unroll=4)


def forward_kernel(grid, pattern_ref, sizes_ref, owner_ref, both_ref, down_ref, htile_ref, *refs):
    outer, inner = grid
    out_refs = refs[-inner - 3 : -3]
    slab_refs = refs[: -inner - 3]
    mixed, product, placed = refs[-3:]
    blocks, slots = pattern_ref.shape
    rows = both_ref.shape[0] // 2
    ens_ref = both_ref.at[rows:]
    width = htile_ref.shape[1]
    extended = jnp.concatenate([both_ref[:rows]] + [ref[...] for ref in slab_refs], axis=0)
    dims = (((0,), (0,)), ((), ()))
    summed = lax.dot_general(down_ref[0], extended, dims, preferred_element_type=jnp.float32)
    summed = summed + lax.dot_general(
        down_ref[1], extended, dims, preferred_element_type=jnp.float32
    )
    for b in range(blocks):
        mixed[b] = summed[:, b * width : (b + 1) * width].astype(jnp.bfloat16)

    def spread(b, carry):
        picked = jnp.concatenate([mixed[pattern_ref[b, k]] for k in range(slots)], axis=1)
        localized = jnp.dot(picked, htile_ref[...], preferred_element_type=jnp.float32)
        columns = pl.ds(pl.multiple_of(b * width, width), width)
        product[b] = localized * ens_ref[:, columns].astype(jnp.float32)
        return carry

    lax.fori_loop(0, blocks, spread, 0, unroll=min(blocks, 8))
    product[blocks] = jnp.zeros((rows, width), jnp.float32)
    lane = lax.broadcasted_iota(jnp.int32, (rows, width), 1)
    me = lax.axis_index("wide")
    here, line = me % inner, me // inner

    def place(owner, block, shift, size):
        both = jnp.where(lane >= shift, product[block], product[block + 1])
        turned = pltpu.roll(both, (width - shift) % width, 1)
        kept = jnp.where(lane < size, turned, 0.0).astype(jnp.bfloat16)
        placed[(owner % inner - here + inner) % inner, (owner // inner - line + outer) % outer] = kept

    region_loop(sizes_ref, owner_ref, width, place)
    for i in range(inner):
        out_refs[i][...] = placed[i]


def scale_kernel(grid, sizes_ref, owner_ref, ens_ref, *refs):
    outer, inner = grid
    cot_refs = refs[:inner]
    out_ref, gathered, columns_of = refs[inner:]
    rows, width = cot_refs[0].shape[1:]
    blocks = ens_ref.shape[1] // width
    lane = lax.broadcasted_iota(jnp.int32, (rows, width), 1)
    me = lax.axis_index("wide")
    here, line = me % inner, me // inner
    for i in range(inner):
        gathered[i] = cot_refs[i][...]
    columns_of[0] = jnp.zeros((rows, width), jnp.float32)

    def place(owner, block, shift, size):
        region = gathered[(here - owner % inner + inner) % inner, (line - owner // inner + outer) % outer]
        turned = pltpu.roll(region.astype(jnp.float32), shift, 1)
        columns_of[block] = jnp.where(lane >= shift, turned, columns_of[block])
        columns_of[block + 1] = turned

    region_loop(sizes_ref, owner_ref, width, place)
    for b in range(blocks):
        part = slice(b * width, (b + 1) * width)
        out_ref[:, part] = (ens_ref[:, part].astype(jnp.float32) * columns_of[b]).astype(
            jnp.bfloat16
        )


def backward_kernel(pattern_ref, up_ref, htile_ref, *refs):
    slab_refs = refs[:-3]
    out_ref, mixed, total = refs[-3:]
    blocks, slots = pattern_ref.shape
    rows = out_ref.shape[0]
    width = htile_ref.shape[1]
    extended = jnp.concatenate([ref[...] for ref in slab_refs], axis=0)
    summed = jnp.dot(up_ref[0], extended, preferred_element_type=jnp.float32)
    summed = summed + jnp.dot(up_ref[1], extended, preferred_element_type=jnp.float32)
    for b in range(blocks):
        mixed[b] = summed[:, b * width : (b + 1) * width].astype(jnp.bfloat16)
        total[b] = jnp.zeros((rows, width), jnp.float32)

    def gather(b, carry):
        spread = lax.dot_general(
            mixed[b], htile_ref[...], (((1,), (1,)), ((), ())), preferred_element_type=jnp.float32
        )
        for k in range(slots):
            target = pattern_ref[b, k]
            total[target] = total[target] + spread[:, k * width : (k + 1) * width]
        return carry

    lax.fori_loop(0, blocks, gather, 0, unroll=min(blocks, 8))
    for b in range(blocks):
        out_ref[:, b * width : (b + 1) * width] = total[b].astype(jnp.bfloat16)


def partial_kernel(*refs):
    count = refs[0].shape[0]
    parts, outs = refs[:-count], refs[-count:]
    for i in range(count):
        total = parts[0][i].astype(jnp.float32)
        for part in parts[1:]:
            total = total + part[i].astype(jnp.float32)
        outs[i][...] = total.astype(outs[i].dtype)


def total_kernel(scale, *refs):
    total = refs[0][...].astype(jnp.float32)
    for part in refs[1:-1]:
        total = total + part[...].astype(jnp.float32)
    refs[-1][...] = (total * scale).astype(jnp.bfloat16)


PARAMS = pltpu.CompilerParams(vmem_limit_bytes=8 << 20)


def cost(flops, moved):
    return pl.CostEstimate(flops=flops, bytes_accessed=moved, transcendentals=0)


def body(alpha, ens, htile, vloc, pattern, region_sizes, owner, cotangent):
    members, fields, levels, columns = alpha.shape
    assert members == 1
    slots, width, _ = htile.shape
    blocks = columns // width
    assert cotangent.shape[2] == width == LANES
    wide = lax.axis_size("wide")
    slabs = lax.axis_size("lev")
    inner = next(i for i in range(math.isqrt(wide), wide + 1) if wide % i == 0)
    outer = wide // inner
    grid = (outer, inner)
    rows = fields * levels
    span = rows * len(slab_steps(slabs))
    member_scale = 1.0 / math.sqrt(members * wide)
    bf16 = functools.partial(jax.ShapeDtypeStruct, dtype=jnp.bfloat16)

    def along_line(value, step):
        pairs = [
            (o * inner + i, (o + step) % outer * inner + i)
            for o in range(outer)
            for i in range(inner)
        ]
        return lax.ppermute(value, "wide", pairs)

    def in_plane(value, step):
        pairs = [
            (o * inner + i, o * inner + (i + step) % inner)
            for o in range(outer)
            for i in range(inner)
        ]
        return lax.ppermute(value, "wide", pairs)

    alpha_rows = alpha.reshape(rows, columns)
    ens_rows = ens.reshape(rows, columns)
    stacked = htile.reshape(slots * width, width)
    alpha_slabs = [alpha_rows] + neighbour_slabs(alpha_rows)

    cot_rows = cotangent.reshape(rows, width)
    cot_line = jnp.stack([cot_rows] + [along_line(cot_rows, i) for i in range(1, outer)])
    cot_parts = [cot_line] + [in_plane(cot_line, i) for i in range(1, inner)]

    both = lax.concatenate([alpha_rows, ens_rows], 0)
    down, up = pl.pallas_call(
        functools.partial(weight_kernel, fields, slabs),
        out_shape=(bf16((2, span, rows)), bf16((2, rows, span))),
        in_specs=[VMEM],
        out_specs=(VMEM, VMEM),
        scratch_shapes=[pltpu.VMEM((2 * 8, LANES), jnp.float32)],
        compiler_params=PARAMS,
        cost_estimate=cost(10**6, 10**5),
        name="weights",
    )(vloc.T)

    sent = pl.pallas_call(
        functools.partial(forward_kernel, grid),
        out_shape=[bf16((outer, rows, width))] * inner,
        in_specs=[SMEM] * 3 + [VMEM] * (2 + len(alpha_slabs)),
        out_specs=[VMEM] * inner,
        scratch_shapes=[
            pltpu.VMEM((blocks, rows, width), jnp.bfloat16),
            pltpu.VMEM((blocks + 1, rows, width), jnp.float32),
            pltpu.VMEM((inner, outer, rows, width), jnp.bfloat16),
        ],
        compiler_params=PARAMS,
        cost_estimate=cost(10**9, 2 << 20),
        name="forward",
    )(pattern, region_sizes, owner, both, down, stacked, *alpha_slabs[1:])

    arrived = [sent[0]] + [in_plane(sent[i], i) for i in range(1, inner)]
    partial = pl.pallas_call(
        partial_kernel,
        out_shape=[bf16((rows, width))] * outer,
        in_specs=[VMEM] * inner,
        out_specs=[VMEM] * outer,
        compiler_params=PARAMS,
        cost_estimate=cost(10**6, 1 << 20),
        name="partial",
    )(*arrived)
    terms = [partial[0]] + [along_line(partial[i], i) for i in range(1, outer)]

    scaled = pl.pallas_call(
        functools.partial(scale_kernel, grid),
        out_shape=bf16((rows, columns)),
        in_specs=[SMEM] * 2 + [VMEM] * (1 + inner),
        out_specs=VMEM,
        scratch_shapes=[
            pltpu.VMEM((inner, outer, rows, width), jnp.bfloat16),
            pltpu.VMEM((blocks + 1, rows, width), jnp.float32),
        ],
        compiler_params=PARAMS,
        cost_estimate=cost(10**7, 1 << 20),
        name="scale",
    )(region_sizes, owner, ens_rows, *cot_parts)
    scaled_slabs = [scaled] + neighbour_slabs(scaled)
    gradient = pl.pallas_call(
        backward_kernel,
        out_shape=bf16((rows, columns)),
        in_specs=[SMEM] + [VMEM] * (2 + len(scaled_slabs)),
        out_specs=VMEM,
        scratch_shapes=[
            pltpu.VMEM((blocks, rows, width), jnp.bfloat16),
            pltpu.VMEM((blocks, rows, width), jnp.float32),
        ],
        compiler_params=PARAMS,
        cost_estimate=cost(10**9, 1 << 20),
        name="backward",
    )(pattern, up, stacked, *scaled_slabs)

    increment = pl.pallas_call(
        functools.partial(total_kernel, member_scale),
        out_shape=bf16((rows, width)),
        in_specs=[VMEM] * outer,
        out_specs=VMEM,
        compiler_params=PARAMS,
        cost_estimate=cost(10**6, 1 << 18),
        name="total",
    )(*terms)
    return (
        increment.reshape(fields, levels, width),
        gradient.reshape(members, fields, levels, columns),
    )


def solution(mesh):
    placed = (
        P("wide", None, "lev", None),
        P("wide", None, "lev", None),
        P(),
        P(),
        P(),
        P(),
        P(),
        P(None, "lev", "wide"),
    )
    return jax.shard_map(
        body,
        mesh=mesh,
        in_specs=placed,
        out_specs=(P(None, "lev", "wide"), P("wide", None, "lev", None)),
        check_vma=False,
    )
```

```python
import functools
import math

import jax
import jax.numpy as jnp
from jax import lax
from jax.experimental import pallas as pl
from jax.experimental.pallas import tpu as pltpu
from jax.sharding import PartitionSpec as P


VREACH = 4
LANES = 128
VMEM = pl.BlockSpec(memory_space=pltpu.VMEM)
ANY = pl.BlockSpec(memory_space=pl.ANY)


def neighbour_slabs(block):
    count = lax.axis_size("lev")
    if count == 2:
        return [lax.ppermute(block, "lev", [(0, 1), (1, 0)])]
    return [
        lax.ppermute(block, "lev", [(i, i + 1) for i in range(count - 1)]),
        lax.ppermute(block, "lev", [(i + 1, i) for i in range(count - 1)]),
    ]


def slab_steps(slabs):
    if slabs == 2:
        return [0, 1 - 2 * lax.axis_index("lev")]
    return [0, -1, 1]


def can_pair(count):
    return count & (count - 1) == 0


def plane_target(index, step, count):
    return index ^ step if can_pair(count) else (index + step) % count


def plane_step(source, target, count):
    return source ^ target if can_pair(count) else (target - source + count) % count


def line_step(source, target, count):
    return (target - source + count) % count


def split_bf16(value):
    high = value.astype(jnp.bfloat16)
    return high, (value - high.astype(jnp.float32)).astype(jnp.bfloat16)


def vertical_weights(fields, slabs, vloc_ref, down_ref, up_ref, taps):
    slab = lax.axis_index("lev")
    reach = VREACH
    levels = vloc_ref.shape[1] // slabs
    rows = fields * levels
    taps[...] = jnp.zeros_like(taps)
    taps[: vloc_ref.shape[0], : vloc_ref.shape[1]] = vloc_ref[...]
    lane = lax.broadcasted_iota(jnp.int32, taps.shape, 1)

    def slab_weights(step):
        first = (slab + step) * levels
        turned = pltpu.roll(taps[...], lax.rem(2 * LANES - first, LANES), 1)
        once = jnp.where(lane < levels, turned, 0.0)
        total = once
        for field in range(1, fields):
            total = total + pltpu.roll(once, field * levels, 1)
        return total

    row = lax.broadcasted_iota(jnp.int32, (rows, rows), 0)
    col = lax.broadcasted_iota(jnp.int32, (rows, rows), 1)
    same = (row // levels) == (col // levels)
    own = slab_weights(0)

    def band(weights, shift, valid):
        total = jnp.zeros((rows, rows), jnp.float32)
        for tap in range(2 * reach + 1):
            line = jnp.broadcast_to(weights[tap : tap + 1, :rows], (rows, rows))
            total = jnp.where(shift == tap - reach, line, total)
        return split_bf16(jnp.where(same & valid, total, 0.0))

    for i, step in enumerate(slab_steps(slabs)):
        valid = (slab + step >= 0) & (slab + step < slabs)
        part = slice(i * rows, (i + 1) * rows)
        offset = step * levels
        down_ref[0, part, :], down_ref[1, part, :] = band(own, row + offset - col, valid)
        up_ref[0, :, part], up_ref[1, :, part] = band(
            own if i == 0 else slab_weights(step), row - col - offset, valid
        )


def start_loads(sources, targets, sems):
    loads = [
        pltpu.make_async_copy(source, target, sems.at[i])
        for i, (source, target) in enumerate(zip(sources, targets))
    ]
    for load in loads:
        load.start()
    return loads


def region_loop(sizes_ref, owner_ref, width, body):
    def step(region, start):
        size = sizes_ref[region]
        body(owner_ref[region], start // width, start % width, size)
        return start + size

    lax.fori_loop(0, sizes_ref.shape[0], step, jnp.int32(0), unroll=4)


def forward_kernel(
    grid, fields, slabs, pattern, sizes, owner, both_ref, vloc_ref, htile_ref, *refs
):
    outer, inner = grid
    pattern_ref, sizes_ref, owner_ref, sems, down_ref, taps, mixed, product, placed = refs[-9:]
    loads = start_loads((pattern, sizes, owner), (pattern_ref, sizes_ref, owner_ref), sems)
    up_ref = refs[-10]
    out_refs = refs[-inner - 10 : -10]
    vertical_weights(fields, slabs, vloc_ref, down_ref, up_ref, taps)
    blocks, slots = pattern_ref.shape
    span, rows = down_ref.shape[1:]
    ens_ref = both_ref.at[span:]
    width = htile_ref.shape[1]
    extended = both_ref[:span]
    dims = (((0,), (0,)), ((), ()))
    summed = lax.dot_general(down_ref[0], extended, dims, preferred_element_type=jnp.float32)
    summed = summed + lax.dot_general(
        down_ref[1], extended, dims, preferred_element_type=jnp.float32
    )
    for b in range(blocks):
        mixed[b] = summed[:, b * width : (b + 1) * width].astype(jnp.bfloat16)

    for load in loads:
        load.wait()

    def spread(b, carry):
        picked = jnp.concatenate([mixed[pattern_ref[b, k]] for k in range(slots)], axis=1)
        localized = jnp.dot(picked, htile_ref[...], preferred_element_type=jnp.float32)
        columns = pl.ds(pl.multiple_of(b * width, width), width)
        product[b] = localized * ens_ref[:, columns].astype(jnp.float32)
        return carry

    lax.fori_loop(0, blocks, spread, 0, unroll=min(blocks, 8))
    product[blocks] = jnp.zeros((rows, width), jnp.float32)
    lane = lax.broadcasted_iota(jnp.int32, (rows, width), 1)
    me = lax.axis_index("wide")
    here, line = me % inner, me // inner

    def place(owner, block, shift, size):
        both = jnp.where(lane >= shift, product[block], product[block + 1])
        turned = pltpu.roll(both, (width - shift) % width, 1)
        kept = jnp.where(lane < size, turned, 0.0).astype(jnp.bfloat16)
        step = plane_step(here, owner % inner, inner), line_step(line, owner // inner, outer)
        placed[step] = kept

    region_loop(sizes_ref, owner_ref, width, place)
    for i in range(inner):
        out_refs[i][...] = placed[i]


def scale_kernel(grid, sizes_ref, owner_ref, ens_ref, *refs):
    outer, inner = grid
    cot_refs = refs[:inner]
    out_ref, gathered, columns_of = refs[inner:]
    rows, width = cot_refs[0].shape[1:]
    blocks = ens_ref.shape[1] // width
    lane = lax.broadcasted_iota(jnp.int32, (rows, width), 1)
    me = lax.axis_index("wide")
    here, line = me % inner, me // inner
    for i in range(inner):
        gathered[i] = cot_refs[i][...]
    columns_of[0] = jnp.zeros((rows, width), jnp.float32)

    def place(owner, block, shift):
        step = plane_step(owner % inner, here, inner), line_step(owner // inner, line, outer)
        region = gathered[step]
        turned = pltpu.roll(region.astype(jnp.float32), shift, 1)
        columns_of[block] = jnp.where(lane >= shift, turned, columns_of[block])
        columns_of[block + 1] = turned

    sizes, owners = sizes_ref[...], owner_ref[...]
    start = jnp.int32(0)
    for region in range(sizes.shape[1]):
        place(owners[0, region], start // width, start % width)
        start = start + sizes[0, region]
    for b in range(blocks):
        part = slice(b * width, (b + 1) * width)
        out_ref[:, part] = (ens_ref[:, part].astype(jnp.float32) * columns_of[b]).astype(
            jnp.bfloat16
        )


def backward_kernel(outer, scale, pattern, up_ref, htile_ref, *refs):
    slab_refs, term_refs = refs[: -outer - 6], refs[-outer - 6 : -6]
    increment_ref, out_ref, pattern_ref, sems, mixed, total = refs[-6:]
    (load,) = start_loads((pattern,), (pattern_ref,), sems)
    summed = term_refs[0][...].astype(jnp.float32)
    for term in term_refs[1:]:
        summed = summed + term[...].astype(jnp.float32)
    increment_ref[...] = (summed * scale).astype(jnp.bfloat16)
    blocks, slots = pattern_ref.shape
    rows = out_ref.shape[0]
    width = htile_ref.shape[1]
    extended = jnp.concatenate([ref[...] for ref in slab_refs], axis=0)
    summed = jnp.dot(up_ref[0], extended, preferred_element_type=jnp.float32)
    summed = summed + jnp.dot(up_ref[1], extended, preferred_element_type=jnp.float32)
    for b in range(blocks):
        mixed[b] = summed[:, b * width : (b + 1) * width].astype(jnp.bfloat16)
        total[b] = jnp.zeros((rows, width), jnp.float32)

    load.wait()

    def gather(b, carry):
        for first in range(0, slots, 2):
            tiles = htile_ref[first * width : (first + 2) * width]
            spread = lax.dot_general(
                mixed[b], tiles, (((1,), (1,)), ((), ())), preferred_element_type=jnp.float32
            )
            for k in range(first, min(first + 2, slots)):
                target = pattern_ref[b, k]
                part = spread[:, (k - first) * width : (k - first + 1) * width]
                total[target] = total[target] + part
        return carry

    lax.fori_loop(0, blocks, gather, 0, unroll=min(blocks, 8))
    for b in range(blocks):
        out_ref[:, b * width : (b + 1) * width] = total[b].astype(jnp.bfloat16)


def partial_kernel(*refs):
    count = refs[0].shape[0]
    parts, outs = refs[:-count], refs[-count:]
    for i in range(count):
        total = parts[0][i].astype(jnp.float32)
        for part in parts[1:]:
            total = total + part[i].astype(jnp.float32)
        outs[i][...] = total.astype(outs[i].dtype)


PARAMS = pltpu.CompilerParams(vmem_limit_bytes=8 << 20)


def cost(flops, moved):
    return pl.CostEstimate(flops=flops, bytes_accessed=moved, transcendentals=0)


def body(alpha, ens, htile, vloc, pattern, region_sizes, owner, cotangent):
    members, fields, levels, columns = alpha.shape
    assert members == 1
    slots, width, _ = htile.shape
    blocks = columns // width
    assert cotangent.shape[2] == width == LANES
    wide = lax.axis_size("wide")
    slabs = lax.axis_size("lev")
    inner = next(i for i in range(math.isqrt(wide), wide + 1) if wide % i == 0)
    outer = wide // inner
    grid = (outer, inner)
    rows = fields * levels
    span = rows * len(slab_steps(slabs))
    member_scale = 1.0 / math.sqrt(members * wide)
    bf16 = functools.partial(jax.ShapeDtypeStruct, dtype=jnp.bfloat16)

    def along_line(value, step):
        pairs = [
            (o * inner + i, (o + step) % outer * inner + i)
            for o in range(outer)
            for i in range(inner)
        ]
        return lax.ppermute(value, "wide", pairs)

    def in_plane(value, step):
        pairs = [
            (o * inner + i, o * inner + plane_target(i, step, inner))
            for o in range(outer)
            for i in range(inner)
        ]
        return lax.ppermute(value, "wide", pairs)

    alpha_rows = alpha.reshape(rows, columns)
    ens_rows = ens.reshape(rows, columns)
    stacked = htile.reshape(slots * width, width)
    alpha_slabs = [alpha_rows] + neighbour_slabs(alpha_rows)

    cot_rows = cotangent.reshape(rows, width)
    cot_line = jnp.stack([cot_rows] + [along_line(cot_rows, i) for i in range(1, outer)])
    cot_parts = [cot_line] + [in_plane(cot_line, i) for i in range(1, inner)]

    both = lax.concatenate([*alpha_slabs, ens_rows], 0)
    sent = pl.pallas_call(
        functools.partial(forward_kernel, grid, fields, slabs),
        out_shape=[bf16((outer, rows, width))] * inner + [bf16((2, rows, span))],
        in_specs=[ANY] * 3 + [VMEM] * 3,
        out_specs=[VMEM] * (inner + 1),
        scratch_shapes=[
            pltpu.SMEM(pattern.shape, jnp.int32),
            pltpu.SMEM(region_sizes.shape, jnp.int32),
            pltpu.SMEM(owner.shape, jnp.int32),
            pltpu.SemaphoreType.DMA((3,)),
            pltpu.VMEM((2, span, rows), jnp.bfloat16),
            pltpu.VMEM((2 * 8, LANES), jnp.float32),
            pltpu.VMEM((blocks, rows, width), jnp.bfloat16),
            pltpu.VMEM((blocks + 1, rows, width), jnp.float32),
            pltpu.VMEM((inner, outer, rows, width), jnp.bfloat16),
        ],
        compiler_params=PARAMS,
        cost_estimate=cost(10**9, 2 << 20),
        name="forward",
    )(pattern, region_sizes, owner, both, vloc.T, stacked)
    *sent, up = sent

    arrived = [sent[0]] + [in_plane(sent[i], i) for i in range(1, inner)]
    partial = pl.pallas_call(
        partial_kernel,
        out_shape=[bf16((rows, width))] * outer,
        in_specs=[VMEM] * inner,
        out_specs=[VMEM] * outer,
        compiler_params=PARAMS,
        cost_estimate=cost(10**6, 1 << 20),
        name="partial",
    )(*arrived)
    terms = [partial[0]] + [along_line(partial[i], i) for i in range(1, outer)]

    scaled = pl.pallas_call(
        functools.partial(scale_kernel, grid),
        out_shape=bf16((rows, columns)),
        in_specs=[VMEM] * 2 + [VMEM] * (1 + inner),
        out_specs=VMEM,
        scratch_shapes=[
            pltpu.VMEM((inner, outer, rows, width), jnp.bfloat16),
            pltpu.VMEM((blocks + 1, rows, width), jnp.float32),
        ],
        compiler_params=PARAMS,
        cost_estimate=cost(10**7, 1 << 20),
        name="scale",
    )(region_sizes[None], owner[None], ens_rows, *cot_parts)
    scaled_slabs = [scaled] + neighbour_slabs(scaled)
    increment, gradient = pl.pallas_call(
        functools.partial(backward_kernel, outer, member_scale),
        out_shape=[bf16((rows, width)), bf16((rows, columns))],
        in_specs=[ANY] + [VMEM] * (2 + len(scaled_slabs) + outer),
        out_specs=[VMEM] * 2,
        scratch_shapes=[
            pltpu.SMEM(pattern.shape, jnp.int32),
            pltpu.SemaphoreType.DMA((1,)),
            pltpu.VMEM((blocks, rows, width), jnp.bfloat16),
            pltpu.VMEM((blocks, rows, width), jnp.float32),
        ],
        compiler_params=PARAMS,
        cost_estimate=cost(10**9, 1 << 20),
        name="backward",
    )(pattern, up, stacked, *scaled_slabs, *terms)

    return (
        increment.reshape(fields, levels, width),
        gradient.reshape(members, fields, levels, columns),
    )


def solution(mesh):
    placed = (
        P("wide", None, "lev", None),
        P("wide", None, "lev", None),
        P(),
        P(),
        P(),
        P(),
        P(),
        P(None, "lev", "wide"),
    )
    return jax.shard_map(
        body,
        mesh=mesh,
        in_specs=placed,
        out_specs=(P(None, "lev", "wide"), P("wide", None, "lev", None)),
        check_vma=False,
    )
```
